32 devices in a mesh: grp: 4 (over y, core), dev: 8 (over z, x).
Axes of the slice: x: 2, y: 2, z: 4, core: 2. Of those that a mesh axis runs over, the one named last changes fastest.
Arguments:
- matrix: float32 [16384, 128], P(('grp', 'dev')), may hold values from -6 to 6
- flip_bits: int32 [16384], P(('grp', 'dev')), may hold values from 0 to 1
- sample_rows: int32 [2048], replicated, may hold values from 0 to 16383
Outputs:
- sketch: float32 [2048, 128], P(('grp', 'dev'))
- gram: float32 [128, 128], replicated
The draws below stay inside these ranges and needn't reach their ends.
Inputs may be any that keep to these rules, and one draw needn't show every extreme that they name: `sample_rows`: rows may repeat.
All inputs are finite; a program needn't handle non-finite values.
Results may differ from the reference program's by a relative error of at most 0.000098.
Values sent between devices are 32-bit elements; how exact they have to be, the bound alone decides.
A program may use at most 64 MiB of HBM per device.

```python
import jax
import jax.numpy as jnp
from jax import lax

F = 128
SAMPLES = 2048
ROWS = 16384


def plant(result, own_key, low, largest):
    shape = result.shape
    spot = [jax.random.randint(jax.random.fold_in(own_key, axis), (), 0, shape[axis]) for axis in range(len(shape))]
    result = result.at[tuple(spot)].set(low)
    longest = shape.index(max(shape))
    spot[longest] = (spot[longest] + 1) % shape[longest]
    return result.at[tuple(spot)].set(largest)


def block_levels(key, extent, shards, smallest, high):
    level = 1.0
    for axis_at, shards_of in shards:
        heights = jax.random.uniform(jax.random.fold_in(jax.random.fold_in(key, 6), axis_at), (shards_of,), jnp.float32, smallest / len(shards), high / len(shards))
        level = level * jnp.repeat(jnp.exp(heights), extent[axis_at] // shards_of).reshape((-1,) + (1,) * (len(extent) - 1 - axis_at))
    return level


def gaussian(stream_key, extent, scale, reach, shards=(), held_as=jnp.bfloat16):
    entries = jax.random.normal(stream_key, extent, jnp.float32) * scale
    if len(shards) > 0:
        entries = block_levels(stream_key, extent, shards, -0.22, 0.18) * entries
    return jnp.clip(entries, min=-reach, max=reach).astype(held_as)


def setup_inputs(seed: int = 0) -> dict:
    seeds = jax.random.split(jax.random.key(seed), 4)
    return {
        "matrix": gaussian(seeds[0], (ROWS, F), 1.0, 6.0, ((0, 32),), jnp.float32),
        "flip_bits": plant(jax.random.randint(seeds[1], (ROWS,), 0, 2), jax.random.fold_in(seeds[1], 1), 0, 1).astype(jnp.int32),
        "sample_rows": plant(jax.random.randint(seeds[2], (SAMPLES,), 0, ROWS), jax.random.fold_in(seeds[2], 1), 0, ROWS - 1).astype(jnp.int32),
    }


def reference(matrix, flip_bits, sample_rows):
    signs = (1 - 2 * flip_bits).astype(jnp.float32)
    mixed = matrix * signs[:, None]
    width = matrix.shape[1]
    half = 1
    for level in range(ROWS.bit_length() - 1):
        cube = mixed.reshape(-1, 2, half, width)
        first = cube[:, 0]
        second = cube[:, 1]
        mixed = jnp.stack([first + second, first - second], axis=1).reshape(ROWS, width)
        half = half * 2
    mixed = mixed / jnp.sqrt(jnp.float32(ROWS))
    sketch = jnp.take(mixed, sample_rows, axis=0)
    gram = jnp.dot(sketch.T, sketch, preferred_element_type=jnp.float32, precision=lax.Precision.HIGHEST) / SAMPLES
    return (sketch, gram)
```

```python
import functools
import math

import jax
import jax.numpy as jnp
from jax import lax
from jax.experimental import pallas as pl
from jax.experimental.pallas import tpu as pltpu
from jax.sharding import PartitionSpec as P

MESH = pl.DeviceIdType.MESH
LANES = 128


def loop(count, fn):
    if count <= 8:
        for step in range(count):
            fn(step)
    else:
        lax.fori_loop(0, count, lambda step, carry: (fn(step), carry)[1], 0)


def parity(bits, width):
    shift = 1
    while shift * 2 < width:
        shift *= 2
    while shift:
        bits = bits ^ (bits >> shift)
        shift //= 2
    return bits & 1


def sign_of(bits, width):
    return (1 - 2 * parity(bits, width)).astype(jnp.float32)


def split3(value):
    high = value.astype(jnp.bfloat16)
    rest = value - high.astype(jnp.float32)
    mid = rest.astype(jnp.bfloat16)
    low = (rest - mid.astype(jnp.float32)).astype(jnp.bfloat16)
    return high, mid, low


def kernel(
    n_grp, n_dev, rows, own,
    x_ref, flip_ref, sample_ref, sketch_ref, gram_ref,
    slabs, flips, cols, index, base, part, blocks, gpart, gslots, gfull, reduced,
    load_sem, pair_send, pair_recv, twin_send, twin_recv, fwd_send, fwd_recv,
    flip_send, flip_recv, rs_send, rs_recv, g_send, g_recv, b_send, b_recv,
):
    f32 = jnp.float32
    devices = n_grp * n_dev
    n_y, n_z = n_grp // 2, n_dev // 2
    groups = n_y * n_z
    chips = devices // 2
    width = x_ref.shape[1]
    pieces = twin_send.shape[0]
    piece = rows // pieces
    samples = sample_ref.shape[0] * LANES
    row_bits = rows.bit_length() - 1
    all_bits = (rows * devices).bit_length() - 1
    me_g, me_d = lax.axis_index("grp"), lax.axis_index("dev")
    core, y = lax.rem(me_g, 2), lax.div(me_g, 2)
    x, z = lax.rem(me_d, 2), lax.div(me_d, 2)
    pair_g = me_g + 1 - 2 * core
    twin_d = me_d + 1 - 2 * x
    mine = y * n_z + z

    def remote(src, dst, send, recv, grp, dev):
        return pltpu.make_async_remote_copy(
            src_ref=src, dst_ref=dst, send_sem=send, recv_sem=recv,
            device_id=(grp, dev), device_id_type=MESH,
        )

    barrier = pltpu.get_barrier_semaphore()

    def greet(i, j):
        pl.semaphore_signal(
            barrier, inc=1,
            device_id=(lax.rem(me_g + i, n_grp), lax.rem(me_d + j, n_dev)),
            device_id_type=MESH,
        )

    for i in range(n_grp):
        loop(n_dev - (i == 0), lambda j: greet(i, j + (i == 0)))

    load = pltpu.make_async_copy(x_ref, slabs.at[0], load_sem)
    load.start()
    pl.semaphore_wait(barrier, devices - 1)

    twin = []
    for c in range(pieces):
        at = pl.ds(c * piece, piece)
        copy = remote(x_ref.at[at], slabs.at[2, at], twin_send.at[c], twin_recv.at[c], me_g, twin_d)
        copy.start()
        twin.append(copy)
    pair = remote(x_ref, slabs.at[1], pair_send, pair_recv, pair_g, me_d)
    pair.start()
    flip_copies = [
        remote(flip_ref, flips.at[0], flip_send.at[0], flip_recv.at[0], pair_g, me_d),
        remote(flip_ref, flips.at[1], flip_send.at[1], flip_recv.at[1], me_g, twin_d),
        remote(flip_ref, flips.at[2], flip_send.at[2], flip_recv.at[2], pair_g, twin_d),
    ]
    for copy in flip_copies:
        copy.start()

    span = n_dev * own // LANES
    for i in range(n_y):
        for r in range(span):
            line = sample_ref[pl.ds((i * 2 + core) * span + r, 1), :]
            cols[pl.ds((i * span + r) * LANES, LANES), :] = jnp.transpose(
                jnp.broadcast_to(line, (LANES, LANES))
            )
    for i in range(n_y):
        for j in range(n_z):
            index[pl.ds((i * n_z + j) * own, own), :] = cols[
                pl.ds((i * n_dev + j * 2 + x) * own, own), :
            ]
    picks = groups * own
    wanted = index[...]
    for k in range(rows // LANES):
        lane = lax.broadcasted_iota(jnp.int32, (picks, LANES), 1) + k * LANES
        base[:, k * LANES:(k + 1) * LANES] = sign_of(wanted & lane, row_bits).astype(jnp.bfloat16)

    def term(slot, flip_bits, grp, dev):
        signs = base[...]
        toggles = (1 - 2 * flip_bits).astype(f32).astype(jnp.bfloat16)
        signs = jnp.concatenate(
            [
                signs[:, k * LANES:(k + 1) * LANES] * toggles[k:k + 1, :]
                for k in range(rows // LANES)
            ],
            axis=1,
        )
        total = None
        for piece_of in split3(slabs[slot]):
            product = jnp.dot(signs, piece_of, preferred_element_type=f32)
            total = product if total is None else total + product
        place = (grp * n_dev + dev) * rows
        return total * sign_of(wanted & place, all_bits)

    load.wait()
    total = term(0, flip_ref[...], me_g, me_d)
    flip_copies[0].wait_recv()
    pair.wait_recv()
    total = total + term(1, flips[0], pair_g, me_d)
    forward = []
    for c in range(pieces):
        at = pl.ds(c * piece, piece)
        twin[c].wait_recv()
        copy = remote(slabs.at[2, at], slabs.at[3, at], fwd_send.at[c], fwd_recv.at[c], pair_g, me_d)
        copy.start()
        forward.append(copy)
    flip_copies[1].wait_recv()
    total = total + term(2, flips[1], me_g, twin_d)
    for copy in forward:
        copy.wait_recv()
    flip_copies[2].wait_recv()
    total = total + term(3, flips[2], pair_g, twin_d)
    part[...] = total.reshape(groups, own, width)

    def give(i, j):
        to_y, to_z = lax.rem(y + i, n_y), lax.rem(z + j, n_z)
        remote(
            part.at[to_y * n_z + to_z], blocks.at[mine], rs_send, rs_recv,
            to_y * 2 + core, to_z * 2 + x,
        ).start()

    for i in range(n_y - 1, -1, -1):
        loop(n_z - (i == 0), lambda j: give(i, j + (i == 0)))
    blocks[mine] = part[mine]
    others = blocks.at[pl.ds(0, groups - 1)]
    pltpu.make_async_copy(others, others, rs_recv).wait()
    sketch = blocks[0]
    for i in range(1, groups):
        sketch = sketch + blocks[i]
    sketch = sketch * (1.0 / math.sqrt(rows * devices))
    sketch_ref[...] = sketch

    chunks = gfull.shape[0]
    stride = chips // chunks
    chunk = width // chunks
    my_chip = y * n_dev + me_d
    linear = me_g * n_dev + me_d
    reducer = (core == 0) & (lax.rem(my_chip, stride) == 0)
    my_chunk = lax.div(my_chip, stride)
    gram = lax.dot_general(
        sketch, sketch, (((0,), (0,)), ((), ())),
        precision=lax.Precision.HIGHEST, preferred_element_type=f32,
    )
    gpart[...] = gram.reshape(chunks, chunk, width)
    for k in range(chunks):
        to_g, to_d = (k * stride) // n_dev * 2, (k * stride) % n_dev

        @pl.when((me_g != to_g) | (me_d != to_d))
        def _():
            remote(gpart.at[k], gslots.at[linear], g_send, g_recv, to_g, to_d).start()

    @pl.when(reducer)
    def _():
        gslots[linear] = gpart[my_chunk]
        rest = gslots.at[pl.ds(0, devices - 1)]
        pltpu.make_async_copy(rest, rest, g_recv).wait()
        result = jnp.sum(gslots[...], axis=0) * (1.0 / samples)
        reduced[...] = result
        gfull[my_chunk] = result

        def tell(i, j):
            remote(
                reduced, gfull.at[my_chunk], b_send, b_recv,
                lax.rem(me_g + i, n_grp), lax.rem(me_d + j, n_dev),
            ).start()

        for i in range(n_grp - 1, -1, -1):
            loop(n_dev - (i == 0), lambda j: tell(i, j + (i == 0)))
        most = gfull.at[pl.ds(0, chunks - 1)]
        pltpu.make_async_copy(most, most, b_recv).wait()
        pltpu.make_async_copy(rest, rest, b_send).wait()
        pltpu.make_async_copy(most, most, g_send).wait()

    @pl.when(jnp.logical_not(reducer))
    def _():
        pltpu.make_async_copy(gfull, gfull, b_recv).wait()
        pltpu.make_async_copy(gfull, gfull, g_send).wait()

    gram_ref[...] = gfull[...].reshape(width, width)
    for copy in twin + forward + flip_copies + [pair]:
        copy.wait_send()
    pltpu.make_async_copy(others, others, rs_send).wait()


def body(matrix, flip_bits, sample_rows):
    rows, width = matrix.shape
    n_grp, n_dev = lax.axis_size("grp"), lax.axis_size("dev")
    devices = n_grp * n_dev
    samples = sample_rows.shape[0]
    own = samples // devices
    groups = devices // 4
    chunks = min(width // 8, devices // 2)
    chunk = width // chunks
    pieces = 4
    f32, i32 = jnp.float32, jnp.int32
    dma = pltpu.SemaphoreType.DMA
    vmem = pl.BlockSpec(memory_space=pltpu.VMEM)
    return pl.pallas_call(
        functools.partial(kernel, n_grp, n_dev, rows, own),
        out_shape=(
            jax.ShapeDtypeStruct((own, width), f32),
            jax.ShapeDtypeStruct((width, width), f32),
        ),
        in_specs=[pl.BlockSpec(memory_space=pl.ANY), vmem, vmem],
        out_specs=(vmem, vmem),
        scratch_shapes=[
            pltpu.VMEM((4, rows, width), f32),
            pltpu.VMEM((3, rows // LANES, LANES), i32),
            pltpu.VMEM((samples // 2, LANES), i32),
            pltpu.VMEM((groups * own, LANES), i32),
            pltpu.VMEM((groups * own, rows), jnp.bfloat16),
            pltpu.VMEM((groups, own, width), f32),
            pltpu.VMEM((groups, own, width), f32),
            pltpu.VMEM((chunks, chunk, width), f32),
            pltpu.VMEM((devices, chunk, width), f32),
            pltpu.VMEM((chunks, chunk, width), f32),
            pltpu.VMEM((chunk, width), f32),
            dma, dma, dma, dma((pieces,)), dma((pieces,)), dma((pieces,)), dma((pieces,)),
            dma((3,)), dma((3,)), dma, dma, dma, dma, dma, dma,
        ],
        compiler_params=pltpu.CompilerParams(collective_id=0, has_side_effects=True),
    )(
        matrix,
        flip_bits.reshape(rows // LANES, LANES),
        sample_rows.reshape(samples // LANES, LANES),
    )


def solution(mesh):
    return jax.shard_map(
        body,
        mesh=mesh,
        in_specs=(P(("grp", "dev"), None), P(("grp", "dev")), P()),
        out_specs=(P(("grp", "dev"), None), P()),
        check_vma=False,
    )
```

```python
import functools
import math

import jax
import jax.numpy as jnp
from jax import lax
from jax.experimental import pallas as pl
from jax.experimental.pallas import tpu as pltpu
from jax.sharding import PartitionSpec as P

MESH = pl.DeviceIdType.MESH
LANES = 128


def loop(count, fn):
    if count <= 8:
        for step in range(count):
            fn(step)
    else:
        lax.fori_loop(0, count, lambda step, carry: (fn(step), carry)[1], 0)


def parity(bits, width):
    shift = 1
    while shift * 2 < width:
        shift *= 2
    while shift:
        bits = bits ^ (bits >> shift)
        shift //= 2
    return bits & 1


def sign_of(bits, width):
    return (1 - 2 * parity(bits, width)).astype(jnp.float32)


def split3(value):
    high = value.astype(jnp.bfloat16)
    rest = value - high.astype(jnp.float32)
    mid = rest.astype(jnp.bfloat16)
    low = (rest - mid.astype(jnp.float32)).astype(jnp.bfloat16)
    return high, mid, low


def kernel(
    n_grp, n_dev, rows, own,
    x_ref, flip_hbm, sample_hbm, sketch_ref, gram_ref,
    flip_ref, sample_ref, slabs, flips, cols, index, base, part, blocks, gpart, gslots, gfull, reduced,
    load_sem, pair_send, pair_recv, twin_send, twin_recv, fwd_send, fwd_recv,
    flip_send, flip_recv, rs_send, rs_recv, g_send, g_recv, b_send, b_recv,
    ready,
):
    f32 = jnp.float32
    devices = n_grp * n_dev
    n_y, n_z = n_grp // 2, n_dev // 2
    groups = n_y * n_z
    width = x_ref.shape[1]
    pieces = twin_send.shape[0]
    piece = rows // pieces
    samples = sample_hbm.shape[0] * LANES
    row_bits = rows.bit_length() - 1
    all_bits = (rows * devices).bit_length() - 1
    me_g, me_d = lax.axis_index("grp"), lax.axis_index("dev")
    core, y = lax.rem(me_g, 2), lax.div(me_g, 2)
    x, z = lax.rem(me_d, 2), lax.div(me_d, 2)
    pair_g = me_g + 1 - 2 * core
    twin_d = me_d + 1 - 2 * x
    mine = y * n_z + z

    def remote(src, dst, send, recv, grp, dev):
        return pltpu.make_async_remote_copy(
            src_ref=src, dst_ref=dst, send_sem=send, recv_sem=recv,
            device_id=(grp, dev), device_id_type=MESH,
        )

    barrier = pltpu.get_barrier_semaphore()

    def signal(sem, grp, dev):
        pl.semaphore_signal(sem, inc=1, device_id=(grp, dev), device_id_type=MESH)

    def along_y(step):
        return me_g + 2 * step, me_d

    def along_z(step):
        return me_g, me_d + 2 * step

    def tell_line(sem, at, size, reach, along):
        for step in range(1, min(reach, size - 1) + 1):
            @pl.when(at >= step)
            def _():
                signal(sem, *along(-step))

            @pl.when(at + step < size)
            def _():
                signal(sem, *along(step))

    def line_count(at, size, reach):
        return jnp.minimum(at, reach) + jnp.minimum(size - 1 - at, reach)

    signal(barrier, pair_g, me_d)
    signal(barrier, me_g, twin_d)
    tell_line(barrier, y, n_y, 1, along_y)
    tell_line(barrier, z, n_z, 1, along_z)

    loads = [
        pltpu.make_async_copy(sample_hbm, sample_ref, load_sem.at[0]),
        pltpu.make_async_copy(flip_hbm, flip_ref, load_sem.at[1]),
        pltpu.make_async_copy(x_ref, slabs.at[0], load_sem.at[2]),
    ]
    for copy in loads:
        copy.start()
    pl.semaphore_wait(barrier, 2 + line_count(y, n_y, 1) + line_count(z, n_z, 1))

    rounds = []
    for at, size, along in ((z, n_z, along_z), (y, n_y, along_y)):
        reach = 1
        while reach < size - 1:
            rounds.append((at, size, reach, along))
            reach *= 2
    rounds.append((y, n_y, n_y - 1, along_y))

    def open_round(k):
        if k < len(rounds):
            at, size, reach, along = rounds[k]
            tell_line(ready.at[k], at, size, reach, along)
        elif k == len(rounds):
            signal(ready.at[k], me_g, twin_d)
        else:
            signal(ready.at[k], pair_g, me_d)

    def close_round(k):
        if k < len(rounds):
            at, size, reach, along = rounds[k]
            pl.semaphore_wait(ready.at[k], line_count(at, size, reach))
        else:
            pl.semaphore_wait(ready.at[k], 1)

    twin = []
    for c in range(pieces):
        at = pl.ds(c * piece, piece)
        copy = remote(x_ref.at[at], slabs.at[2, at], twin_send.at[c], twin_recv.at[c], me_g, twin_d)
        copy.start()
        twin.append(copy)
    pair = remote(x_ref, slabs.at[1], pair_send, pair_recv, pair_g, me_d)
    pair.start()
    flip_copies = [
        remote(flip_ref, flips.at[0], flip_send.at[0], flip_recv.at[0], pair_g, me_d),
        remote(flip_ref, flips.at[1], flip_send.at[1], flip_recv.at[1], me_g, twin_d),
        remote(flips.at[1], flips.at[2], flip_send.at[2], flip_recv.at[2], pair_g, me_d),
    ]
    open_round(0)
    for copy in loads:
        copy.wait()
    for copy in flip_copies[:2]:
        copy.start()

    span = n_dev * own // LANES
    for i in range(n_y):
        for r in range(span):
            line = sample_ref[pl.ds((i * 2 + core) * span + r, 1), :]
            cols[pl.ds((i * span + r) * LANES, LANES), :] = jnp.transpose(
                jnp.broadcast_to(line, (LANES, LANES))
            )
    for i in range(n_y):
        for j in range(n_z):
            index[pl.ds((i * n_z + j) * own, own), :] = cols[
                pl.ds((i * n_dev + j * 2 + x) * own, own), :
            ]
    close_round(0)
    open_round(1)
    picks = groups * own
    wanted = index[...]
    for k in range(rows // LANES):
        lane = lax.broadcasted_iota(jnp.int32, (picks, LANES), 1) + k * LANES
        base[:, k * LANES:(k + 1) * LANES] = sign_of(wanted & lane, row_bits).astype(jnp.bfloat16)

    def term(slot, flip_bits, grp, dev):
        signs = base[...]
        toggles = (1 - 2 * flip_bits).astype(f32).astype(jnp.bfloat16)
        signs = jnp.concatenate(
            [
                signs[:, k * LANES:(k + 1) * LANES] * toggles[k:k + 1, :]
                for k in range(rows // LANES)
            ],
            axis=1,
        )
        total = None
        for piece_of in split3(slabs[slot]):
            product = jnp.dot(signs, piece_of, preferred_element_type=f32)
            total = product if total is None else total + product
        place = (grp * n_dev + dev) * rows
        return total * sign_of(wanted & place, all_bits)

    for k in range(1, len(rounds) - 1):
        close_round(k)
        open_round(k + 1)
    total = term(0, flip_ref[...], me_g, me_d)
    close_round(len(rounds) - 1)
    open_round(len(rounds))
    flip_copies[0].wait_recv()
    pair.wait_recv()
    total = total + term(1, flips[0], pair_g, me_d)
    forward = []
    for c in range(pieces):
        at = pl.ds(c * piece, piece)
        twin[c].wait_recv()
        copy = remote(slabs.at[2, at], slabs.at[3, at], fwd_send.at[c], fwd_recv.at[c], pair_g, me_d)
        copy.start()
        forward.append(copy)
    flip_copies[1].wait_recv()
    flip_copies[2].start()
    close_round(len(rounds))
    open_round(len(rounds) + 1)
    total = total + term(2, flips[1], me_g, twin_d)
    for copy in forward:
        copy.wait_recv()
    flip_copies[2].wait_recv()
    total = total + term(3, flips[2], pair_g, twin_d)
    part[...] = total.reshape(groups, own, width)

    def give(i, j):
        to_y, to_z = lax.rem(y + i, n_y), lax.rem(z + j, n_z)
        remote(
            part.at[to_y * n_z + to_z], blocks.at[mine], rs_send, rs_recv,
            to_y * 2 + core, to_z * 2 + x,
        ).start()

    for i in range(n_y - 1, -1, -1):
        loop(n_z - (i == 0), lambda j: give(i, j + (i == 0)))
    blocks[mine] = part[mine]
    others = blocks.at[pl.ds(0, groups - 1)]
    pltpu.make_async_copy(others, others, rs_recv).wait()
    sketch = blocks[0]
    for i in range(1, groups):
        sketch = sketch + blocks[i]
    sketch = sketch * (1.0 / math.sqrt(rows * devices))
    sketch_ref[...] = sketch

    close_round(len(rounds) + 1)
    chunks = gfull.shape[0]
    across = min(chunks, n_dev // 2)
    first = (n_dev - across) // 2
    chunk = width // chunks
    linear = me_g * n_dev + me_d
    reducer = (me_g < chunks // across) & (me_d >= first) & (me_d < first + across)
    my_chunk = me_g * across + me_d - first
    gram = lax.dot_general(
        sketch, sketch, (((0,), (0,)), ((), ())),
        precision=lax.Precision.HIGHEST, preferred_element_type=f32,
    )
    gpart[...] = gram.reshape(chunks, chunk, width)
    for k in range(chunks):
        to_g, to_d = k // across, first + k % across

        @pl.when((me_g != to_g) | (me_d != to_d))
        def _():
            remote(gpart.at[k], gslots.at[linear], g_send, g_recv, to_g, to_d).start()

    @pl.when(reducer)
    def _():
        gslots[linear] = gpart[my_chunk]
        rest = gslots.at[pl.ds(0, devices - 1)]
        pltpu.make_async_copy(rest, rest, g_recv).wait()
        result = jnp.sum(gslots[...], axis=0) * (1.0 / samples)
        reduced[...] = result
        gfull[my_chunk] = result

        def tell(i, j):
            remote(
                reduced, gfull.at[my_chunk], b_send, b_recv,
                lax.rem(me_g + i, n_grp), lax.rem(me_d + j, n_dev),
            ).start()

        for i in range(n_grp - 1, -1, -1):
            loop(n_dev - (i == 0), lambda j: tell(i, j + (i == 0)))
        most = gfull.at[pl.ds(0, chunks - 1)]
        pltpu.make_async_copy(most, most, b_recv).wait()
        pltpu.make_async_copy(rest, rest, b_send).wait()
        pltpu.make_async_copy(most, most, g_send).wait()

    @pl.when(jnp.logical_not(reducer))
    def _():
        pltpu.make_async_copy(gfull, gfull, b_recv).wait()
        pltpu.make_async_copy(gfull, gfull, g_send).wait()

    gram_ref[...] = gfull[...].reshape(width, width)
    for copy in twin + forward + flip_copies + [pair]:
        copy.wait_send()
    pltpu.make_async_copy(others, others, rs_send).wait()


def body(matrix, flip_bits, sample_rows):
    rows, width = matrix.shape
    n_grp, n_dev = lax.axis_size("grp"), lax.axis_size("dev")
    devices = n_grp * n_dev
    samples = sample_rows.shape[0]
    own = samples // devices
    groups = devices // 4
    chunks = min(width // 8, devices // 2)
    chunk = width // chunks
    pieces = 4
    f32, i32 = jnp.float32, jnp.int32
    dma = pltpu.SemaphoreType.DMA
    vmem = pl.BlockSpec(memory_space=pltpu.VMEM)
    return pl.pallas_call(
        functools.partial(kernel, n_grp, n_dev, rows, own),
        out_shape=(
            pltpu.VMEM((own, width), f32),
            pltpu.VMEM((width, width), f32),
        ),
        in_specs=[pl.BlockSpec(memory_space=pl.ANY)] * 3,
        out_specs=(vmem, vmem),
        scratch_shapes=[
            pltpu.VMEM((rows // LANES, LANES), i32),
            pltpu.VMEM((samples // LANES, LANES), i32),
            pltpu.VMEM((4, rows, width), f32),
            pltpu.VMEM((3, rows // LANES, LANES), i32),
            pltpu.VMEM((samples // 2, LANES), i32),
            pltpu.VMEM((groups * own, LANES), i32),
            pltpu.VMEM((groups * own, rows), jnp.bfloat16),
            pltpu.VMEM((groups, own, width), f32),
            pltpu.VMEM((groups, own, width), f32),
            pltpu.VMEM((chunks, chunk, width), f32),
            pltpu.VMEM((devices, chunk, width), f32),
            pltpu.VMEM((chunks, chunk, width), f32),
            pltpu.VMEM((chunk, width), f32),
            dma((3,)), dma, dma, dma((pieces,)), dma((pieces,)), dma((pieces,)), dma((pieces,)),
            dma((3,)), dma((3,)), dma, dma, dma, dma, dma, dma,
            pltpu.SemaphoreType.REGULAR((16,)),
        ],
        compiler_params=pltpu.CompilerParams(collective_id=0, has_side_effects=True),
    )(
        matrix,
        flip_bits.reshape(rows // LANES, LANES),
        sample_rows.reshape(samples // LANES, LANES),
    )


def solution(mesh):
    return jax.shard_map(
        body,
        mesh=mesh,
        in_specs=(P(("grp", "dev"), None), P(("grp", "dev")), P()),
        out_specs=(P(("grp", "dev"), None), P()),
        check_vma=False,
    )
```

```python
import functools
import math

import jax
import jax.numpy as jnp
from jax import lax
from jax.experimental import pallas as pl
from jax.experimental.pallas import tpu as pltpu
from jax.sharding import PartitionSpec as P

MESH = pl.DeviceIdType.MESH
LANES = 128


def loop(count, fn):
    if count <= 8:
        for step in range(count):
            fn(step)
    else:
        lax.fori_loop(0, count, lambda step, carry: (fn(step), carry)[1], 0)


def parity(bits, width):
    shift = 1
    while shift * 2 < width:
        shift *= 2
    while shift:
        bits = bits ^ (bits >> shift)
        shift //= 2
    return bits & 1


def sign_of(bits, width):
    return (1 - 2 * parity(bits, width)).astype(jnp.float32)


def split3(value):
    high = value.astype(jnp.bfloat16)
    rest = value - high.astype(jnp.float32)
    mid = rest.astype(jnp.bfloat16)
    low = (rest - mid.astype(jnp.float32)).astype(jnp.bfloat16)
    return high, mid, low


def kernel(
    n_grp, n_dev, rows, own,
    x_ref, flip_hbm, sample_hbm, sketch_ref, gram_ref,
    flip_ref, sample_ref, x_full, slabs, flips, cols, index, base, part, blocks, gpart, gslots, gfull, reduced,
    load_sem, pair_send, pair_recv, twin_send, twin_recv, fwd_send, fwd_recv,
    flip_send, flip_recv, rs_send, rs_recv, g_send, g_recv, b_send, b_recv,
    ready,
):
    f32 = jnp.float32
    devices = n_grp * n_dev
    n_y, n_z = n_grp // 2, n_dev // 2
    groups = n_y * n_z
    width = x_ref.shape[1]
    pieces = twin_send.shape[0]
    piece = rows // pieces
    samples = sample_hbm.shape[0] * LANES
    row_bits = rows.bit_length() - 1
    all_bits = (rows * devices).bit_length() - 1
    me_g, me_d = lax.axis_index("grp"), lax.axis_index("dev")
    core, y = lax.rem(me_g, 2), lax.div(me_g, 2)
    x, z = lax.rem(me_d, 2), lax.div(me_d, 2)
    pair_g = me_g + 1 - 2 * core
    twin_d = me_d + 1 - 2 * x
    mine = y * n_z + z

    def remote(src, dst, send, recv, grp, dev):
        return pltpu.make_async_remote_copy(
            src_ref=src, dst_ref=dst, send_sem=send, recv_sem=recv,
            device_id=(grp, dev), device_id_type=MESH,
        )

    barrier = pltpu.get_barrier_semaphore()

    def signal(sem, grp, dev):
        pl.semaphore_signal(sem, inc=1, device_id=(grp, dev), device_id_type=MESH)

    def along_y(step):
        return me_g + 2 * step, me_d

    def along_z(step):
        return me_g, me_d + 2 * step

    def tell_line(sem, at, size, reach, along):
        for step in range(1, min(reach, size - 1) + 1):
            @pl.when(at >= step)
            def _():
                signal(sem, *along(-step))

            @pl.when(at + step < size)
            def _():
                signal(sem, *along(step))

    def line_count(at, size, reach):
        return jnp.minimum(at, reach) + jnp.minimum(size - 1 - at, reach)

    signal(barrier, pair_g, me_d)
    signal(barrier, me_g, twin_d)
    tell_line(barrier, y, n_y, 1, along_y)
    tell_line(barrier, z, n_z, 1, along_z)

    loads = [
        pltpu.make_async_copy(sample_hbm, sample_ref, load_sem.at[0]),
        pltpu.make_async_copy(flip_hbm, flip_ref, load_sem.at[1]),
        pltpu.make_async_copy(x_ref, x_full, load_sem.at[2]),
    ]
    for copy in loads:
        copy.start()
    pl.semaphore_wait(barrier, 2 + line_count(y, n_y, 1) + line_count(z, n_z, 1))

    rounds = []
    for at, size, along in ((z, n_z, along_z), (y, n_y, along_y)):
        reach = 1
        while reach < size - 1:
            rounds.append((at, size, reach, along))
            reach *= 2
    rounds.append((y, n_y, n_y - 1, along_y))

    def open_round(k):
        if k < len(rounds):
            at, size, reach, along = rounds[k]
            tell_line(ready.at[k], at, size, reach, along)
        elif k == len(rounds):
            signal(ready.at[k], me_g, twin_d)
        else:
            signal(ready.at[k], pair_g, me_d)

    def close_round(k):
        if k < len(rounds):
            at, size, reach, along = rounds[k]
            pl.semaphore_wait(ready.at[k], line_count(at, size, reach))
        else:
            pl.semaphore_wait(ready.at[k], 1)

    half = width // 2
    left = lax.broadcasted_iota(jnp.int32, (1, width), 1) < half

    def swap(value):
        return pltpu.roll(value, half, value.ndim - 1)

    for copy in loads:
        copy.wait()
    top, bottom = x_full[pl.ds(0, rows // 2), :], x_full[pl.ds(rows // 2, rows // 2), :]
    slabs[0, 0] = jnp.where(left, top, swap(bottom))
    slabs[1, 0] = jnp.where(left, swap(top), bottom)
    twin, pair = [], []
    for h in range(2):
        for c in range(pieces // 2):
            at = pl.ds(c * piece, piece)
            k = h * (pieces // 2) + c
            copy = remote(
                slabs.at[h, 0, at], slabs.at[h, 2, at],
                twin_send.at[k], twin_recv.at[k], me_g, twin_d,
            )
            copy.start()
            twin.append(copy)
    for h in range(2):
        copy = remote(
            slabs.at[h, 0], slabs.at[h, 1], pair_send.at[h], pair_recv.at[h], pair_g, me_d
        )
        copy.start()
        pair.append(copy)
    flip_copies = [
        remote(flip_ref, flips.at[0], flip_send.at[0], flip_recv.at[0], pair_g, me_d),
        remote(flip_ref, flips.at[1], flip_send.at[1], flip_recv.at[1], me_g, twin_d),
        remote(flips.at[1], flips.at[2], flip_send.at[2], flip_recv.at[2], pair_g, me_d),
    ]
    open_round(0)
    for copy in flip_copies[:2]:
        copy.start()

    span = n_dev * own // LANES
    for i in range(n_y):
        for r in range(span):
            line = sample_ref[pl.ds((i * 2 + core) * span + r, 1), :]
            cols[pl.ds((i * span + r) * LANES, LANES), :] = jnp.transpose(
                jnp.broadcast_to(line, (LANES, LANES))
            )
    for i in range(n_y):
        for j in range(n_z):
            index[pl.ds((i * n_z + j) * own, own), :] = cols[
                pl.ds((i * n_dev + j * 2 + x) * own, own), :
            ]
    close_round(0)
    open_round(1)
    picks = groups * own
    wanted = index[...]
    for k in range(rows // LANES):
        lane = lax.broadcasted_iota(jnp.int32, (picks, LANES), 1) + k * LANES
        base[:, k * LANES:(k + 1) * LANES] = sign_of(wanted & lane, row_bits).astype(jnp.bfloat16)

    def term(h, slot, flip_bits, grp, dev):
        signs = base[...]
        toggles = (1 - 2 * flip_bits).astype(f32).astype(jnp.bfloat16)
        signs = jnp.concatenate(
            [
                signs[:, k * LANES:(k + 1) * LANES] * toggles[k:k + 1, :]
                for k in range(rows // LANES)
            ],
            axis=1,
        )
        packed = slabs[h, slot]
        high, mid, low = split3(packed)
        high_s, mid_s, low_s = split3(swap(packed))
        right = jnp.concatenate(
            [
                jnp.concatenate([jnp.where(left, high, mid_s), low], axis=1),
                jnp.concatenate([jnp.where(left, high_s, mid), low_s], axis=1),
            ],
            axis=0,
        )
        product = jnp.dot(signs, right, preferred_element_type=f32)
        first, last = product[:, :width], product[:, width:]
        place = (grp * n_dev + dev) * rows
        return (first + swap(first) + last) * sign_of(wanted & place, all_bits)

    def give(h, i, j):
        to_y, to_z = lax.rem(y + i, n_y), lax.rem(z + j, n_z)
        remote(
            part.at[h, to_y * n_z + to_z], blocks.at[h, mine], rs_send.at[h], rs_recv.at[h],
            to_y * 2 + core, to_z * 2 + x,
        ).start()

    for k in range(1, len(rounds) - 1):
        close_round(k)
        open_round(k + 1)
    totals = [term(h, 0, flip_ref[...], me_g, me_d) for h in range(2)]
    close_round(len(rounds) - 1)
    open_round(len(rounds))
    flip_copies[0].wait_recv()
    for h in range(2):
        pair[h].wait_recv()
        totals[h] = totals[h] + term(h, 1, flips[0], pair_g, me_d)
    flip_copies[1].wait_recv()
    flip_copies[2].start()
    forward = []
    for h in range(2):
        for c in range(pieces // 2):
            at = pl.ds(c * piece, piece)
            k = h * (pieces // 2) + c
            twin[k].wait_recv()
            copy = remote(
                slabs.at[h, 2, at], slabs.at[h, 3, at],
                fwd_send.at[k], fwd_recv.at[k], pair_g, me_d,
            )
            copy.start()
            forward.append(copy)
        total = totals[h] + term(h, 2, flips[1], me_g, twin_d)
        if h == 0:
            flip_copies[2].wait_recv()
        for copy in forward[h * (pieces // 2):]:
            copy.wait_recv()
        total = total + term(h, 3, flips[2], pair_g, twin_d)
        total = total.reshape(groups, own, width)
        part[h] = jnp.where(
            left.reshape(1, 1, width), total[:, :own // 2], swap(total[:, own // 2:])
        )
        if h == 0:
            close_round(len(rounds))
            open_round(len(rounds) + 1)
        for i in range(n_y - 1, -1, -1):
            loop(n_z - (i == 0), lambda j: give(h, i, j + (i == 0)))
        blocks[h, mine] = part[h, mine]
    sums = []
    for h in range(2):
        others = blocks.at[h, pl.ds(0, groups - 1)]
        pltpu.make_async_copy(others, others, rs_recv.at[h]).wait()
        summed = blocks[h, 0]
        for i in range(1, groups):
            summed = summed + blocks[h, i]
        sums.append(summed)
    sketch = jnp.concatenate(
        [
            jnp.where(left, sums[0], swap(sums[1])),
            jnp.where(left, swap(sums[0]), sums[1]),
        ],
        axis=0,
    )
    sketch = sketch * (1.0 / math.sqrt(rows * devices))
    sketch_ref[...] = sketch

    close_round(len(rounds) + 1)
    chunks = gfull.shape[0]
    across = min(chunks, n_dev // 2)
    first = (n_dev - across) // 2
    chunk = width // chunks
    linear = me_g * n_dev + me_d
    reducer = (me_g < chunks // across) & (me_d >= first) & (me_d < first + across)
    my_chunk = me_g * across + me_d - first
    gram = lax.dot_general(
        sketch, sketch, (((0,), (0,)), ((), ())),
        precision=lax.Precision.HIGHEST, preferred_element_type=f32,
    )
    gpart[...] = gram.reshape(chunks, chunk, width)
    turn = lax.rem(linear, chunks)
    for k in range(chunks):
        to = lax.rem(k + turn, chunks)
        to_g, to_d = lax.div(to, across), first + lax.rem(to, across)

        @pl.when((me_g != to_g) | (me_d != to_d))
        def _():
            remote(gpart.at[to], gslots.at[linear], g_send, g_recv, to_g, to_d).start()

    @pl.when(reducer)
    def _():
        gslots[linear] = gpart[my_chunk]
        rest = gslots.at[pl.ds(0, devices - 1)]
        pltpu.make_async_copy(rest, rest, g_recv).wait()
        result = jnp.sum(gslots[...], axis=0) * (1.0 / samples)
        reduced[...] = result
        gfull[my_chunk] = result

        def tell(i, j):
            remote(
                reduced, gfull.at[my_chunk], b_send, b_recv,
                lax.rem(me_g + i, n_grp), lax.rem(me_d + j, n_dev),
            ).start()

        for i in range(n_grp - 1, -1, -1):
            loop(n_dev - (i == 0), lambda j: tell(i, j + (i == 0)))
        most = gfull.at[pl.ds(0, chunks - 1)]
        pltpu.make_async_copy(most, most, b_recv).wait()
        pltpu.make_async_copy(rest, rest, b_send).wait()
        pltpu.make_async_copy(most, most, g_send).wait()

    @pl.when(jnp.logical_not(reducer))
    def _():
        pltpu.make_async_copy(gfull, gfull, b_recv).wait()
        pltpu.make_async_copy(gfull, gfull, g_send).wait()

    gram_ref[...] = gfull[...].reshape(width, width)
    for copy in twin + forward + flip_copies + pair:
        copy.wait_send()
    for h in range(2):
        others = blocks.at[h, pl.ds(0, groups - 1)]
        pltpu.make_async_copy(others, others, rs_send.at[h]).wait()


def body(matrix, flip_bits, sample_rows):
    rows, width = matrix.shape
    n_grp, n_dev = lax.axis_size("grp"), lax.axis_size("dev")
    devices = n_grp * n_dev
    samples = sample_rows.shape[0]
    own = samples // devices
    groups = devices // 4
    chunks = min(width // 8, devices // 2)
    chunk = width // chunks
    pieces = 4
    f32, i32 = jnp.float32, jnp.int32
    dma = pltpu.SemaphoreType.DMA
    vmem = pl.BlockSpec(memory_space=pltpu.VMEM)
    return pl.pallas_call(
        functools.partial(kernel, n_grp, n_dev, rows, own),
        out_shape=(
            pltpu.VMEM((own, width), f32),
            pltpu.VMEM((width, width), f32),
        ),
        in_specs=[pl.BlockSpec(memory_space=pl.ANY)] * 3,
        out_specs=(vmem, vmem),
        scratch_shapes=[
            pltpu.VMEM((rows // LANES, LANES), i32),
            pltpu.VMEM((samples // LANES, LANES), i32),
            pltpu.VMEM((rows, width), f32),
            pltpu.VMEM((2, 4, rows // 2, width), f32),
            pltpu.VMEM((3, rows // LANES, LANES), i32),
            pltpu.VMEM((samples // 2, LANES), i32),
            pltpu.VMEM((groups * own, LANES), i32),
            pltpu.VMEM((groups * own, rows), jnp.bfloat16),
            pltpu.VMEM((2, groups, own // 2, width), f32),
            pltpu.VMEM((2, groups, own // 2, width), f32),
            pltpu.VMEM((chunks, chunk, width), f32),
            pltpu.VMEM((devices, chunk, width), f32),
            pltpu.VMEM((chunks, chunk, width), f32),
            pltpu.VMEM((chunk, width), f32),
            dma((3,)), dma((2,)), dma((2,)), dma((pieces,)), dma((pieces,)), dma((pieces,)), dma((pieces,)),
            dma((3,)), dma((3,)), dma((2,)), dma((2,)), dma, dma, dma, dma,
            pltpu.SemaphoreType.REGULAR((16,)),
        ],
        compiler_params=pltpu.CompilerParams(collective_id=0, has_side_effects=True),
    )(
        matrix,
        flip_bits.reshape(rows // LANES, LANES),
        sample_rows.reshape(samples // LANES, LANES),
    )


def solution(mesh):
    return jax.shard_map(
        body,
        mesh=mesh,
        in_specs=(P(("grp", "dev"), None), P(("grp", "dev")), P()),
        out_specs=(P(("grp", "dev"), None), P()),
        check_vma=False,
    )
```

```python
import functools
import math

import jax
import jax.numpy as jnp
from jax import lax
from jax.experimental import pallas as pl
from jax.experimental.pallas import tpu as pltpu
from jax.sharding import PartitionSpec as P

MESH = pl.DeviceIdType.MESH
LANES = 128


def loop(count, fn):
    if count <= 8:
        for step in range(count):
            fn(step)
    else:
        lax.fori_loop(0, count, lambda step, carry: (fn(step), carry)[1], 0)


def parity(bits, width):
    shift = 1
    while shift * 2 < width:
        shift *= 2
    while shift:
        bits = bits ^ (bits >> shift)
        shift //= 2
    return bits & 1


def sign_of(bits, width):
    return (1 - 2 * parity(bits, width)).astype(jnp.float32)


def split3(value):
    high = value.astype(jnp.bfloat16)
    rest = value - high.astype(jnp.float32)
    mid = rest.astype(jnp.bfloat16)
    low = (rest - mid.astype(jnp.float32)).astype(jnp.bfloat16)
    return high, mid, low


def kernel(
    n_grp, n_dev, rows, own,
    x_ref, flip_hbm, sample_hbm, sketch_ref, gram_ref,
    flip_ref, sample_ref, x_full, slabs, flips, cols, index, base, part, blocks, gpart, gslots, gfull, reduced,
    load_sem, pair_send, pair_recv, twin_send, twin_recv, fwd_send, fwd_recv,
    flip_send, flip_recv, rs_send, rs_recv, g_send, g_recv, b_send, b_recv,
    ready,
):
    f32 = jnp.float32
    devices = n_grp * n_dev
    n_y, n_z = n_grp // 2, n_dev // 2
    groups = n_y * n_z
    width = x_ref.shape[1]
    pieces = twin_send.shape[0]
    piece = rows // pieces
    samples = sample_hbm.shape[0] * LANES
    row_bits = rows.bit_length() - 1
    all_bits = (rows * devices).bit_length() - 1
    me_g, me_d = lax.axis_index("grp"), lax.axis_index("dev")
    core, y = lax.rem(me_g, 2), lax.div(me_g, 2)
    x, z = lax.rem(me_d, 2), lax.div(me_d, 2)
    pair_g = me_g + 1 - 2 * core
    twin_d = me_d + 1 - 2 * x
    mine = y * n_z + z

    def remote(src, dst, send, recv, grp, dev):
        return pltpu.make_async_remote_copy(
            src_ref=src, dst_ref=dst, send_sem=send, recv_sem=recv,
            device_id=(grp, dev), device_id_type=MESH,
        )

    barrier = pltpu.get_barrier_semaphore()

    def signal(sem, grp, dev):
        pl.semaphore_signal(sem, inc=1, device_id=(grp, dev), device_id_type=MESH)

    def along_y(step):
        return me_g + 2 * step, me_d

    def along_z(step):
        return me_g, me_d + 2 * step

    def tell_line(sem, at, size, reach, along):
        for step in range(1, min(reach, size - 1) + 1):
            @pl.when(at >= step)
            def _():
                signal(sem, *along(-step))

            @pl.when(at + step < size)
            def _():
                signal(sem, *along(step))

    def line_count(at, size, reach):
        return jnp.minimum(at, reach) + jnp.minimum(size - 1 - at, reach)

    signal(barrier, pair_g, me_d)
    signal(barrier, me_g, twin_d)
    tell_line(barrier, y, n_y, 1, along_y)
    tell_line(barrier, z, n_z, 1, along_z)

    loads = [
        pltpu.make_async_copy(sample_hbm, sample_ref, load_sem.at[0]),
        pltpu.make_async_copy(flip_hbm, flip_ref, load_sem.at[1]),
        pltpu.make_async_copy(x_ref, x_full, load_sem.at[2]),
    ]
    for copy in loads:
        copy.start()
    pl.semaphore_wait(barrier, 2 + line_count(y, n_y, 1) + line_count(z, n_z, 1))

    rounds = []
    for at, size, along in ((z, n_z, along_z), (y, n_y, along_y)):
        reach = 1
        while reach < size - 1:
            rounds.append((at, size, reach, along))
            reach *= 2
    rounds.append((y, n_y, n_y - 1, along_y))

    def open_round(k):
        if k < len(rounds):
            at, size, reach, along = rounds[k]
            tell_line(ready.at[k], at, size, reach, along)
        elif k == len(rounds):
            signal(ready.at[k], me_g, twin_d)
        else:
            signal(ready.at[k], pair_g, me_d)

    def close_round(k):
        if k < len(rounds):
            at, size, reach, along = rounds[k]
            pl.semaphore_wait(ready.at[k], line_count(at, size, reach))
        else:
            pl.semaphore_wait(ready.at[k], 1)

    half = width // 2
    left = lax.broadcasted_iota(jnp.int32, (1, width), 1) < half

    def swap(value):
        return pltpu.roll(value, half, value.ndim - 1)

    for copy in loads:
        copy.wait()
    top, bottom = x_full[pl.ds(0, rows // 2), :], x_full[pl.ds(rows // 2, rows // 2), :]
    slabs[0, 0] = jnp.where(left, top, swap(bottom))
    slabs[1, 0] = jnp.where(left, swap(top), bottom)
    twin, pair = [], []
    for h in range(2):
        for c in range(pieces // 2):
            at = pl.ds(c * piece, piece)
            k = h * (pieces // 2) + c
            copy = remote(
                slabs.at[h, 0, at], slabs.at[h, 2, at],
                twin_send.at[k], twin_recv.at[k], me_g, twin_d,
            )
            copy.start()
            twin.append(copy)
    for h in range(2):
        copy = remote(
            slabs.at[h, 0], slabs.at[h, 1], pair_send.at[h], pair_recv.at[h], pair_g, me_d
        )
        copy.start()
        pair.append(copy)
    flip_copies = [
        remote(flip_ref, flips.at[0], flip_send.at[0], flip_recv.at[0], pair_g, me_d),
        remote(flip_ref, flips.at[1], flip_send.at[1], flip_recv.at[1], me_g, twin_d),
        remote(flips.at[1], flips.at[2], flip_send.at[2], flip_recv.at[2], pair_g, me_d),
    ]
    open_round(0)
    for copy in flip_copies[:2]:
        copy.start()

    span = n_dev * own // LANES
    for i in range(n_y):
        for r in range(span):
            line = sample_ref[pl.ds((i * 2 + core) * span + r, 1), :]
            cols[pl.ds((i * span + r) * LANES, LANES), :] = jnp.transpose(
                jnp.broadcast_to(line, (LANES, LANES))
            )
    for i in range(n_y):
        for j in range(n_z):
            index[pl.ds((i * n_z + j) * own, own), :] = cols[
                pl.ds((i * n_dev + j * 2 + x) * own, own), :
            ]
    close_round(0)
    open_round(1)
    picks = groups * own
    wanted = index[...]
    for k in range(rows // LANES):
        lane = lax.broadcasted_iota(jnp.int32, (picks, LANES), 1) + k * LANES
        base[:, k * LANES:(k + 1) * LANES] = sign_of(wanted & lane, row_bits).astype(jnp.bfloat16)

    owner_signs = [
        sign_of(wanted & ((grp * n_dev + dev) * rows), all_bits)
        for grp, dev in ((me_g, me_d), (pair_g, me_d), (me_g, twin_d), (pair_g, twin_d))
    ]

    def term(h, slot, flip_bits, grp, dev):
        signs = base[...]
        toggles = (1 - 2 * flip_bits).astype(f32).astype(jnp.bfloat16)
        signs = jnp.concatenate(
            [
                signs[:, k * LANES:(k + 1) * LANES] * toggles[k:k + 1, :]
                for k in range(rows // LANES)
            ],
            axis=1,
        )
        packed = slabs[h, slot]
        high, mid, low = split3(packed)
        high_s, mid_s, low_s = split3(swap(packed))
        right = jnp.concatenate(
            [
                jnp.concatenate([jnp.where(left, high, mid_s), low], axis=1),
                jnp.concatenate([jnp.where(left, high_s, mid), low_s], axis=1),
            ],
            axis=0,
        )
        product = jnp.dot(signs, right, preferred_element_type=f32)
        first, last = product[:, :width], product[:, width:]
        return (first + swap(first) + last) * owner_signs[slot]

    def give(h, i, j):
        to_y, to_z = lax.rem(y + i, n_y), lax.rem(z + j, n_z)
        remote(
            part.at[h, to_y * n_z + to_z], blocks.at[h, mine], rs_send.at[h], rs_recv.at[h],
            to_y * 2 + core, to_z * 2 + x,
        ).start()

    for k in range(1, len(rounds) - 1):
        close_round(k)
        open_round(k + 1)
    totals = [term(h, 0, flip_ref[...], me_g, me_d) for h in range(2)]
    close_round(len(rounds) - 1)
    open_round(len(rounds))
    flip_copies[0].wait_recv()
    for h in range(2):
        pair[h].wait_recv()
        totals[h] = totals[h] + term(h, 1, flips[0], pair_g, me_d)
    flip_copies[1].wait_recv()
    flip_copies[2].start()
    forward = []
    for h in range(2):
        for c in range(pieces // 2):
            at = pl.ds(c * piece, piece)
            k = h * (pieces // 2) + c
            twin[k].wait_recv()
            copy = remote(
                slabs.at[h, 2, at], slabs.at[h, 3, at],
                fwd_send.at[k], fwd_recv.at[k], pair_g, me_d,
            )
            copy.start()
            forward.append(copy)
        total = totals[h] + term(h, 2, flips[1], me_g, twin_d)
        if h == 0:
            flip_copies[2].wait_recv()
        for copy in forward[h * (pieces // 2):]:
            copy.wait_recv()
        total = total + term(h, 3, flips[2], pair_g, twin_d)
        total = total.reshape(groups, own, width)
        part[h] = jnp.where(
            left.reshape(1, 1, width), total[:, :own // 2], swap(total[:, own // 2:])
        )
        if h == 0:
            close_round(len(rounds))
            open_round(len(rounds) + 1)
        for i in range(n_y - 1, -1, -1):
            loop(n_z - (i == 0), lambda j: give(h, i, j + (i == 0)))
        blocks[h, mine] = part[h, mine]
    sums = []
    for h in range(2):
        others = blocks.at[h, pl.ds(0, groups - 1)]
        pltpu.make_async_copy(others, others, rs_recv.at[h]).wait()
        summed = blocks[h, 0]
        for i in range(1, groups):
            summed = summed + blocks[h, i]
        sums.append(summed)
    sketch = jnp.concatenate(
        [
            jnp.where(left, sums[0], swap(sums[1])),
            jnp.where(left, swap(sums[0]), sums[1]),
        ],
        axis=0,
    )
    sketch = sketch * (1.0 / math.sqrt(rows * devices))
    sketch_ref[...] = sketch

    close_round(len(rounds) + 1)
    chunks = gfull.shape[0]
    across = min(chunks, n_dev // 2)
    first = (n_dev - across) // 2
    chunk = width // chunks
    linear = me_g * n_dev + me_d
    reducer = (me_g < chunks // across) & (me_d >= first) & (me_d < first + across)
    my_chunk = me_g * across + me_d - first
    gram = lax.dot_general(
        sketch, sketch, (((0,), (0,)), ((), ())),
        precision=lax.Precision.HIGHEST, preferred_element_type=f32,
    )
    gpart[...] = gram.reshape(chunks, chunk, width)
    turn = lax.rem(linear, chunks)
    for k in range(chunks):
        to = lax.rem(k + turn, chunks)
        to_g, to_d = lax.div(to, across), first + lax.rem(to, across)

        @pl.when((me_g != to_g) | (me_d != to_d))
        def _():
            remote(gpart.at[to], gslots.at[linear], g_send, g_recv, to_g, to_d).start()

    @pl.when(reducer)
    def _():
        gslots[linear] = gpart[my_chunk]
        rest = gslots.at[pl.ds(0, devices - 1)]
        pltpu.make_async_copy(rest, rest, g_recv).wait()
        result = jnp.sum(gslots[...], axis=0) * (1.0 / samples)
        reduced[...] = result
        gfull[my_chunk] = result

        def tell(i, j):
            remote(
                reduced, gfull.at[my_chunk], b_send, b_recv,
                lax.rem(me_g + i, n_grp), lax.rem(me_d + j, n_dev),
            ).start()

        for i in range(n_grp - 1, -1, -1):
            loop(n_dev - (i == 0), lambda j: tell(i, j + (i == 0)))
        most = gfull.at[pl.ds(0, chunks - 1)]
        pltpu.make_async_copy(most, most, b_recv).wait()
        pltpu.make_async_copy(rest, rest, b_send).wait()
        pltpu.make_async_copy(most, most, g_send).wait()

    @pl.when(jnp.logical_not(reducer))
    def _():
        pltpu.make_async_copy(gfull, gfull, b_recv).wait()
        pltpu.make_async_copy(gfull, gfull, g_send).wait()

    gram_ref[...] = gfull[...].reshape(width, width)
    for copy in twin + forward + flip_copies + pair:
        copy.wait_send()
    for h in range(2):
        others = blocks.at[h, pl.ds(0, groups - 1)]
        pltpu.make_async_copy(others, others, rs_send.at[h]).wait()


def body(matrix, flip_bits, sample_rows):
    rows, width = matrix.shape
    n_grp, n_dev = lax.axis_size("grp"), lax.axis_size("dev")
    devices = n_grp * n_dev
    samples = sample_rows.shape[0]
    own = samples // devices
    groups = devices // 4
    chunks = min(width // 8, devices // 2)
    chunk = width // chunks
    pieces = 4
    f32, i32 = jnp.float32, jnp.int32
    dma = pltpu.SemaphoreType.DMA
    vmem = pl.BlockSpec(memory_space=pltpu.VMEM)
    return pl.pallas_call(
        functools.partial(kernel, n_grp, n_dev, rows, own),
        out_shape=(
            pltpu.VMEM((own, width), f32),
            pltpu.VMEM((width, width), f32),
        ),
        in_specs=[pl.BlockSpec(memory_space=pl.ANY)] * 3,
        out_specs=(vmem, vmem),
        scratch_shapes=[
            pltpu.VMEM((rows // LANES, LANES), i32),
            pltpu.VMEM((samples // LANES, LANES), i32),
            pltpu.VMEM((rows, width), f32),
            pltpu.VMEM((2, 4, rows // 2, width), f32),
            pltpu.VMEM((3, rows // LANES, LANES), i32),
            pltpu.VMEM((samples // 2, LANES), i32),
            pltpu.VMEM((groups * own, LANES), i32),
            pltpu.VMEM((groups * own, rows), jnp.bfloat16),
            pltpu.VMEM((2, groups, own // 2, width), f32),
            pltpu.VMEM((2, groups, own // 2, width), f32),
            pltpu.VMEM((chunks, chunk, width), f32),
            pltpu.VMEM((devices, chunk, width), f32),
            pltpu.VMEM((chunks, chunk, width), f32),
            pltpu.VMEM((chunk, width), f32),
            dma((3,)), dma((2,)), dma((2,)), dma((pieces,)), dma((pieces,)), dma((pieces,)), dma((pieces,)),
            dma((3,)), dma((3,)), dma((2,)), dma((2,)), dma, dma, dma, dma,
            pltpu.SemaphoreType.REGULAR((16,)),
        ],
        compiler_params=pltpu.CompilerParams(collective_id=0, has_side_effects=True),
    )(
        matrix,
        flip_bits.reshape(rows // LANES, LANES),
        sample_rows.reshape(samples // LANES, LANES),
    )


def solution(mesh):
    return jax.shard_map(
        body,
        mesh=mesh,
        in_specs=(P(("grp", "dev"), None), P(("grp", "dev")), P()),
        out_specs=(P(("grp", "dev"), None), P()),
        check_vma=False,
    )
```
